32 devices in a mesh: blk: 8 (over z, y), exp: 4 (over x, core).
Axes of the slice: x: 2, y: 2, z: 4, core: 2. Of those that a mesh axis runs over, the one named last changes fastest.
Arguments:
- grad_block: bfloat16 [128, 256, 2048], P('exp', 'blk'), may hold values from -6 to 6
- momentum: float32 [128, 256, 2048], P('exp', 'blk'), may hold values from -6 to 6
- model_root: bfloat16 [2048, 2048], P('blk'), may hold values from -0.125 to 0.125
- expert_root: bfloat16 [128, 128], replicated, may hold values from -0.5 to 0.5
Outputs:
- momentum_new: float32 [128, 256, 2048], P('exp', 'blk')
The draws below stay inside these ranges and needn't reach their ends.
All inputs are finite; a program needn't handle non-finite values.
Results may differ from the reference program's by a relative error of at most 0.0031.
Values may be sent and summed in bfloat16 or wider, within the bound.
A program may use at most 128 MiB of HBM per device.

```python
import jax
import jax.numpy as jnp

D = 2048
HW = 256
EXPERTS = 128


def levels(rng, dims, cuts, low, largest):
    level, own = 1.0, jax.random.fold_in(rng, 6)
    for dim, shards_of in cuts:
        steps = jnp.exp(jax.random.uniform(jax.random.fold_in(own, dim), (shards_of,), jnp.float32, low / len(cuts), largest / len(cuts)))
        level = level * jnp.repeat(steps, dims[dim] // shards_of).reshape([-1 if axis == dim else 1 for axis in range(len(dims))])
    return level


def bell_draw(stream_key, shape, deviation, most, split=(), held_as=jnp.bfloat16):
    values = deviation * jax.random.normal(stream_key, shape, jnp.float32)
    if split:
        values = values * levels(stream_key, shape, split, -0.22, 0.18)
    return jnp.clip(values, -most, most).astype(held_as)


def setup_inputs(seed: int = 0) -> dict:
    streams_of = jax.random.split(jax.random.key(seed), 5)
    grad_block = bell_draw(streams_of[0], (EXPERTS, HW, D), 1.0, 6.0, ((0, 4), (1, 8)))
    momentum = bell_draw(streams_of[1], (EXPERTS, HW, D), 1.0, 6.0, ((0, 4), (1, 8)), jnp.float32)
    model_root = bell_draw(streams_of[2], (D, D), D ** -0.5, 0.125, ((0, 8),))
    expert_root = bell_draw(streams_of[3], (EXPERTS, EXPERTS), EXPERTS ** -0.5, 0.5)
    return dict(grad_block=grad_block, momentum=momentum, model_root=model_root, expert_root=expert_root)


def reference(grad_block, momentum, model_root, expert_root):
    experts, hidden, width = grad_block.shape
    flat_rows = grad_block.reshape(experts * hidden, width)
    model_mode = jnp.dot(flat_rows, model_root.T, preferred_element_type=jnp.float32).astype(jnp.bfloat16)
    stacked = model_mode.reshape(experts, hidden * width)
    expert_mode = jnp.dot(expert_root, stacked, preferred_element_type=jnp.float32).astype(jnp.bfloat16)
    expert_mode = expert_mode.reshape(experts, hidden, width)
    return 0.9 * momentum + expert_mode.astype(jnp.float32)
```

```python
import functools

import jax
import jax.numpy as jnp
from jax import lax
from jax.experimental import pallas as pl
from jax.experimental.pallas import tpu as pltpu
from jax.sharding import PartitionSpec as P

MESH = pl.DeviceIdType.MESH
SUB = 16
TILE = 256


def kernel(
    n_blk, n_exp, n_chunks,
    grad, momentum, root_rows, expert_root, out,
    gathered, root, mix, blended, total,
    x_send, x_recv, p_send, p_recv, f_send, f_recv, own_sem,
    z_send, z_recv, y_send, y_recv, c_send, c_recv, root_sem, mom_sem, out_sem,
):
    local_experts, local_hidden, width = grad.shape
    groups = local_hidden // SUB
    chunk = width // n_chunks
    chips = n_exp // 2
    n_z = n_blk // 2
    rows = local_experts * SUB
    half = root.shape[2]
    slice_rows = 2 * half

    me = lax.axis_index("exp")
    chip, core = me // 2, me % 2
    blk = lax.axis_index("blk")
    zi, yi = blk // 2, blk % 2
    mate = {"exp": chip * 2 + 1 - core}
    y_peer = {"blk": zi * 2 + 1 - yi}

    def chip_at(offset):
        return lax.rem(chip + offset + chips, chips)

    def z_at(offset):
        return lax.rem(zi + offset + n_z, n_z)

    def remote(src, dst, send, recv, device):
        return pltpu.make_async_remote_copy(
            src_ref=src, dst_ref=dst, send_sem=send, recv_sem=recv, device_id=device, device_id_type=MESH
        )

    barrier = pltpu.get_barrier_semaphore()
    peers = [mate, y_peer]
    peers += [{"exp": chip_at(c) * 2 + core} for c in range(1, chips)]
    peers += [{"blk": z_at(d) * 2 + yi} for d in range(1, n_z)]
    for peer in peers:
        pl.semaphore_signal(barrier, inc=1, device_id=peer, device_id_type=MESH)
    pl.semaphore_wait(barrier, len(peers))

    pieces = [(g, c) for g in range(groups) for c in range(n_chunks)]
    grad_at = [grad.at[:, pl.ds(g * SUB, SUB), pl.ds(c * chunk, chunk)] for g, c in pieces]

    def x_copy(p, off):
        slot = gathered.at[p, me]
        return remote(grad_at[p], slot, x_send.at[p, off - 1], x_recv.at[p, off - 1], {"exp": chip_at(off) * 2 + core})

    def p_copy(p):
        return remote(grad_at[p], gathered.at[p, me], p_send.at[p], p_recv.at[p], mate)

    def f_copy(p, off):
        slot = gathered.at[p, chip_at(-off) * 2 + core]
        return remote(slot, slot, f_send.at[p, off - 1], f_recv.at[p, off - 1], mate)

    def own_copy(p):
        return pltpu.make_async_copy(grad_at[p], gathered.at[p, me], own_sem.at[p])

    own_half = root_rows.at[core]

    def z_copy(d):
        return remote(own_half, root.at[blk, core], z_send.at[d - 1], z_recv.at[d - 1], {"blk": z_at(d) * 2 + yi})

    def y_copy(d):
        slot = root.at[z_at(-d) * 2 + yi, core]
        return remote(own_half if d == 0 else slot, slot, y_send.at[d], y_recv.at[d], y_peer)

    def c_copy(side, d):
        slot = root.at[z_at(-d) * 2 + (yi if side == 0 else 1 - yi), core]
        return remote(slot, slot, c_send.at[side, d], c_recv.at[side, d], mate)

    root_own = pltpu.make_async_copy(root_rows, root.at[blk], root_sem)

    def mom_copy(g):
        return pltpu.make_async_copy(momentum.at[:, pl.ds(g * SUB, SUB), :], total.at[g], mom_sem.at[g])

    def out_copy(g, b):
        cols = pl.ds(pl.multiple_of(b * slice_rows, slice_rows), slice_rows)
        return pltpu.make_async_copy(
            total.at[g, :, :, cols], out.at[:, pl.ds(g * SUB, SUB), cols], out_sem.at[g, b]
        )

    for off in range(1, chips):
        x_copy(0, off).start()
    y_copy(0).start()
    for d in range(1, n_z):
        z_copy(d).start()
    for p in range(1, len(pieces)):
        for off in range(1, chips):
            x_copy(p, off).start()
    for p in range(len(pieces)):
        own_copy(p).start()
        p_copy(p).start()
    root_own.start()
    for g in range(groups):
        mom_copy(g).start()

    experts = expert_root.shape[1]
    spread = lax.broadcasted_iota(jnp.int32, (rows, local_experts), 0) // SUB
    spread = spread == lax.broadcasted_iota(jnp.int32, (rows, local_experts), 1)
    mine = expert_root[pl.ds(pl.multiple_of(me * local_experts, local_experts), local_experts), :]
    tall = jnp.dot(jnp.where(spread, 1.0, 0.0).astype(jnp.bfloat16), mine, preferred_element_type=jnp.float32)
    tall = tall.astype(jnp.bfloat16)

    @pl.loop(0, experts * SUB // TILE)
    def _(t):
        col = t * TILE + lax.broadcasted_iota(jnp.int32, (experts, TILE), 1)
        pick = col // SUB == lax.broadcasted_iota(jnp.int32, (experts, TILE), 0)
        wide = jnp.dot(tall, jnp.where(pick, 1.0, 0.0).astype(jnp.bfloat16), preferred_element_type=jnp.float32)
        same = lax.broadcasted_iota(jnp.int32, (rows, TILE), 0) % SUB == lax.broadcasted_iota(
            jnp.int32, (rows, TILE), 1) % SUB
        mix[:, pl.ds(pl.multiple_of(t * TILE, TILE), TILE)] = jnp.where(same, wide, 0.0).astype(jnp.bfloat16)

    for g in range(groups):
        mom_copy(g).wait()

        @pl.loop(0, local_experts)
        def _(e):
            total[g, e] = 0.9 * total[g, e]

    def blend(p):
        g, c = pieces[p]

        @pl.loop(0, chunk // TILE)
        def _(t):
            block = gathered[p, :, :, :, pl.ds(pl.multiple_of(t * TILE, TILE), TILE)]
            block = block.reshape(experts * SUB, TILE)
            cols = pl.ds(pl.multiple_of(c * chunk + t * TILE, TILE), TILE)
            blended[g, :, cols] = jnp.dot(
                mix[...], block, preferred_element_type=jnp.float32
            ).astype(jnp.bfloat16)

    def apply_root(g, first, last):
        cols = pl.ds(first * chunk, (last - first) * chunk)

        @pl.loop(0, n_blk)
        def _(b):
            taps = root[b, :, :, cols].reshape(slice_rows, (last - first) * chunk)
            part = lax.dot_general(
                blended[g, :, cols], taps, (((1,), (1,)), ((), ())), preferred_element_type=jnp.float32
            )
            dst = pl.ds(pl.multiple_of(b * slice_rows, slice_rows), slice_rows)
            total[g, :, :, dst] += part.reshape(local_experts, SUB, slice_rows)
            if last == n_chunks:
                out_copy(g, b).start()

    def take_z(d):
        z_copy(d).wait_recv()
        y_copy(d).start()
        c_copy(0, d).start()

    def take_y(d):
        y_copy(d).wait_recv()
        c_copy(1, d).start()

    events = [functools.partial(take_z, d) for d in range(1, n_z)]
    events += [functools.partial(take_y, d) for d in range(n_z)]
    ready = len(pieces) * 5 // 8
    done = 0
    pending = 0
    for p, (g, c) in enumerate(pieces):
        for off in range(1, chips):
            x_copy(p, off).wait_recv()
            f_copy(p, off).start()
        goal = len(events) if p >= ready else len(events) * (p + 1) // (ready + 1)
        for event in events[done:goal]:
            event()
        done = goal
        own_copy(p).wait()
        p_copy(p).wait_recv()
        for off in range(1, chips):
            f_copy(p, off).wait_recv()
        blend(p)
        if p == ready:
            root_own.wait()
            for d in range(n_z):
                if d:
                    c_copy(0, d).wait_recv()
                c_copy(1, d).wait_recv()
        if p >= ready:
            while pending <= p:
                gg, first = pieces[pending]
                last = c + 1 if gg == g else n_chunks
                apply_root(gg, first, last)
                pending += last - first

    for p in range(len(pieces)):
        p_copy(p).wait_send()
        for off in range(1, chips):
            x_copy(p, off).wait_send()
            f_copy(p, off).wait_send()
    for d in range(n_z):
        y_copy(d).wait_send()
        c_copy(1, d).wait_send()
        if d:
            z_copy(d).wait_send()
            c_copy(0, d).wait_send()
    for g in range(groups):

        @pl.loop(0, n_blk)
        def _(b):
            out_copy(g, b).wait()


def solution(mesh):
    n_blk, n_exp = mesh.shape["blk"], mesh.shape["exp"]

    def per_device(grad_block, momentum, model_root, expert_root):
        local_experts, local_hidden, width = grad_block.shape
        experts = expert_root.shape[0]
        groups, n_chunks = local_hidden // SUB, 4
        pieces, rows = groups * n_chunks, local_experts * SUB
        half = model_root.shape[0] // 2
        chips, n_z = n_exp // 2, n_blk // 2
        dma = pltpu.SemaphoreType.DMA
        hbm = pl.BlockSpec(memory_space=pl.ANY)
        return pl.pallas_call(
            functools.partial(kernel, n_blk, n_exp, n_chunks),
            out_shape=jax.ShapeDtypeStruct(momentum.shape, jnp.float32),
            in_specs=[hbm, hbm, hbm, pl.BlockSpec(memory_space=pltpu.VMEM)],
            out_specs=hbm,
            scratch_shapes=[
                pltpu.VMEM((pieces, n_exp, local_experts, SUB, width // n_chunks), jnp.bfloat16),
                pltpu.VMEM((n_blk, 2, half, width), jnp.bfloat16),
                pltpu.VMEM((rows, experts * SUB), jnp.bfloat16),
                pltpu.VMEM((groups, rows, width), jnp.bfloat16),
                pltpu.VMEM((groups, local_experts, SUB, width), jnp.float32),
                dma((pieces, chips - 1)), dma((pieces, chips - 1)),
                dma((pieces,)), dma((pieces,)),
                dma((pieces, chips - 1)), dma((pieces, chips - 1)),
                dma((pieces,)),
                dma((n_z - 1,)), dma((n_z - 1,)),
                dma((n_z,)), dma((n_z,)),
                dma((2, n_z)), dma((2, n_z)),
                dma, dma((groups,)), dma((groups, n_blk)),
            ],
            compiler_params=pltpu.CompilerParams(
                collective_id=0, has_side_effects=True, vmem_limit_bytes=67_043_328
            ),
        )(grad_block, momentum, model_root.reshape(2, half, width), expert_root)

    placed = (P("exp", "blk", None), P("exp", "blk", None), P("blk", None), P())
    return jax.shard_map(
        per_device, mesh=mesh, in_specs=placed, out_specs=P("exp", "blk", None), check_vma=False
    )
```

```python
import functools

import jax
import jax.numpy as jnp
from jax import lax
from jax.experimental import pallas as pl
from jax.experimental.pallas import tpu as pltpu
from jax.sharding import PartitionSpec as P

MESH = pl.DeviceIdType.MESH
SUB = 16
TILE = 256


def kernel(
    n_blk, n_exp, n_chunks,
    grad, momentum, root_rows, expert_root, out,
    gathered, root, mix, blended,
    x_send, x_recv, p_send, p_recv, f_send, f_recv, own_sem,
    z_send, z_recv, y_send, y_recv, c_send, c_recv, root_sem, mom_sem,
):
    local_experts, local_hidden, width = grad.shape
    groups = local_hidden // SUB
    chunk = width // n_chunks
    chips = n_exp // 2
    n_z = n_blk // 2
    rows = local_experts * SUB
    half = root.shape[2]
    batch = 4 if n_exp % 4 == 0 else 2
    depth = batch * rows
    slice_rows = 2 * half

    me = lax.axis_index("exp")
    chip, core = me // 2, me % 2
    blk = lax.axis_index("blk")
    zi, yi = blk // 2, blk % 2
    mate = {"exp": chip * 2 + 1 - core}
    y_peer = {"blk": zi * 2 + 1 - yi}

    def chip_at(offset):
        return lax.rem(chip + offset + chips, chips)

    def z_at(offset):
        return lax.rem(zi + offset + n_z, n_z)

    def remote(src, dst, send, recv, device):
        return pltpu.make_async_remote_copy(
            src_ref=src, dst_ref=dst, send_sem=send, recv_sem=recv, device_id=device, device_id_type=MESH
        )

    barrier = pltpu.get_barrier_semaphore()
    peers = [mate, y_peer]
    peers += [{"exp": chip_at(c) * 2 + core} for c in range(1, chips)]
    peers += [{"blk": z_at(d) * 2 + yi} for d in range(1, n_z)]
    for peer in peers:
        pl.semaphore_signal(barrier, inc=1, device_id=peer, device_id_type=MESH)
    pl.semaphore_wait(barrier, len(peers))

    pieces = [(g, c) for g in range(groups) for c in range(n_chunks)]
    grad_at = [grad.at[:, pl.ds(g * SUB, SUB), pl.ds(c * chunk, chunk)] for g, c in pieces]

    def x_copy(p, off):
        slot = gathered.at[p, me]
        return remote(grad_at[p], slot, x_send.at[p, off - 1], x_recv.at[p, off - 1], {"exp": chip_at(off) * 2 + core})

    def p_copy(p):
        return remote(grad_at[p], gathered.at[p, me], p_send.at[p], p_recv.at[p], mate)

    def f_copy(p, off):
        slot = gathered.at[p, chip_at(-off) * 2 + core]
        return remote(slot, slot, f_send.at[p, off - 1], f_recv.at[p, off - 1], mate)

    def own_copy(p):
        return pltpu.make_async_copy(grad_at[p], gathered.at[p, me], own_sem.at[p])

    own_half = root_rows.at[core]

    def z_copy(d):
        return remote(own_half, root.at[blk, core], z_send.at[d - 1], z_recv.at[d - 1], {"blk": z_at(d) * 2 + yi})

    def y_copy(d):
        slot = root.at[z_at(-d) * 2 + yi, core]
        return remote(own_half if d == 0 else slot, slot, y_send.at[d], y_recv.at[d], y_peer)

    def c_copy(side, d):
        slot = root.at[z_at(-d) * 2 + (yi if side == 0 else 1 - yi), core]
        return remote(slot, slot, c_send.at[side, d], c_recv.at[side, d], mate)

    root_own = pltpu.make_async_copy(root_rows, root.at[blk], root_sem)

    def mom_copy(g):
        cols = pl.ds(g * SUB, SUB)
        return pltpu.make_async_copy(momentum.at[:, cols, :], out.at[:, cols, :], mom_sem.at[g])

    for off in range(1, chips):
        x_copy(0, off).start()
    y_copy(0).start()
    for d in range(1, n_z):
        z_copy(d).start()
    for p in range(1, len(pieces)):
        for off in range(1, chips):
            x_copy(p, off).start()
    for p in range(len(pieces)):
        own_copy(p).start()
        p_copy(p).start()
    root_own.start()
    for g in range(groups):
        mom_copy(g).start()

    experts = expert_root.shape[1]
    spread = lax.broadcasted_iota(jnp.int32, (rows, local_experts), 0) // SUB
    spread = spread == lax.broadcasted_iota(jnp.int32, (rows, local_experts), 1)
    mine = expert_root[pl.ds(pl.multiple_of(me * local_experts, local_experts), local_experts), :]
    tall = jnp.dot(jnp.where(spread, 1.0, 0.0).astype(jnp.bfloat16), mine, preferred_element_type=jnp.float32)
    tall = tall.astype(jnp.bfloat16)

    @pl.loop(0, experts * SUB // TILE)
    def _(t):
        col = t * TILE + lax.broadcasted_iota(jnp.int32, (experts, TILE), 1)
        pick = col // SUB == lax.broadcasted_iota(jnp.int32, (experts, TILE), 0)
        wide = jnp.dot(tall, jnp.where(pick, 1.0, 0.0).astype(jnp.bfloat16), preferred_element_type=jnp.float32)
        same = lax.broadcasted_iota(jnp.int32, (rows, TILE), 0) % SUB == lax.broadcasted_iota(
            jnp.int32, (rows, TILE), 1) % SUB
        mix[:, pl.ds(pl.multiple_of(t * TILE, TILE), TILE)] = jnp.where(same, wide, 0.0).astype(jnp.bfloat16)

    for g in range(groups):
        mom_copy(g).wait()

        @pl.loop(0, local_experts)
        def _(e):
            out[e, pl.ds(g * SUB, SUB)] = 0.9 * out[e, pl.ds(g * SUB, SUB)]

    def blend(p):
        g, c = pieces[p]

        @pl.loop(0, chunk // TILE)
        def _(t):
            lanes = pl.ds(pl.multiple_of(t * TILE, TILE), TILE)
            cols = pl.ds(pl.multiple_of(c * chunk + t * TILE, TILE), TILE)

            def term(k):
                block = gathered[p, pl.ds(k * batch, batch), :, :, lanes].reshape(depth, TILE)
                taps = mix[:, pl.ds(pl.multiple_of(k * depth, depth), depth)]
                return jnp.dot(taps, block, preferred_element_type=jnp.float32)

            acc = term(0)
            if n_exp > batch:
                acc = lax.fori_loop(1, n_exp // batch, lambda k, a: a + term(k), acc)
            blended[g, :, cols] = acc.astype(jnp.bfloat16)

    def apply_root(g, first, last):
        cols = pl.ds(first * chunk, (last - first) * chunk)

        @pl.loop(0, n_blk)
        def _(b):
            taps = root[b, :, :, cols].reshape(slice_rows, (last - first) * chunk)
            part = lax.dot_general(
                blended[g, :, cols], taps, (((1,), (1,)), ((), ())), preferred_element_type=jnp.float32
            )
            dst = pl.ds(pl.multiple_of(b * slice_rows, slice_rows), slice_rows)
            out[:, pl.ds(g * SUB, SUB), dst] += part.reshape(local_experts, SUB, slice_rows)

    def take_z(d):
        z_copy(d).wait_recv()
        y_copy(d).start()
        c_copy(0, d).start()

    def take_y(d):
        y_copy(d).wait_recv()
        c_copy(1, d).start()

    events = [functools.partial(take_z, d) for d in range(1, n_z)]
    events += [functools.partial(take_y, d) for d in range(n_z)]
    ready = len(pieces) * 5 // 8
    done = 0
    pending = 0
    for p, (g, c) in enumerate(pieces):
        for off in range(1, chips):
            x_copy(p, off).wait_recv()
            f_copy(p, off).start()
        goal = len(events) if p >= ready else len(events) * (p + 1) // (ready + 1)
        for event in events[done:goal]:
            event()
        done = goal
        own_copy(p).wait()
        p_copy(p).wait_recv()
        for off in range(1, chips):
            f_copy(p, off).wait_recv()
        blend(p)
        if p == ready:
            root_own.wait()
            for d in range(n_z):
                if d:
                    c_copy(0, d).wait_recv()
                c_copy(1, d).wait_recv()
        if p >= ready:
            while pending <= p:
                gg, first = pieces[pending]
                last = c + 1 if gg == g else n_chunks
                apply_root(gg, first, last)
                pending += last - first

    for p in range(len(pieces)):
        p_copy(p).wait_send()
        for off in range(1, chips):
            x_copy(p, off).wait_send()
            f_copy(p, off).wait_send()
    for d in range(n_z):
        y_copy(d).wait_send()
        c_copy(1, d).wait_send()
        if d:
            z_copy(d).wait_send()
            c_copy(0, d).wait_send()


def solution(mesh):
    n_blk, n_exp = mesh.shape["blk"], mesh.shape["exp"]

    def per_device(grad_block, momentum, model_root, expert_root):
        local_experts, local_hidden, width = grad_block.shape
        experts = expert_root.shape[0]
        groups, n_chunks = local_hidden // SUB, 8
        pieces, rows = groups * n_chunks, local_experts * SUB
        half = model_root.shape[0] // 2
        chips, n_z = n_exp // 2, n_blk // 2
        dma = pltpu.SemaphoreType.DMA
        hbm = pl.BlockSpec(memory_space=pl.ANY)
        return pl.pallas_call(
            functools.partial(kernel, n_blk, n_exp, n_chunks),
            out_shape=pltpu.VMEM(momentum.shape, jnp.float32),
            in_specs=[hbm, hbm, hbm, pl.BlockSpec(memory_space=pltpu.VMEM)],
            out_specs=pl.BlockSpec(memory_space=pltpu.VMEM),
            scratch_shapes=[
                pltpu.VMEM((pieces, n_exp, local_experts, SUB, width // n_chunks), jnp.bfloat16),
                pltpu.VMEM((n_blk, 2, half, width), jnp.bfloat16),
                pltpu.VMEM((rows, experts * SUB), jnp.bfloat16),
                pltpu.VMEM((groups, rows, width), jnp.bfloat16),
                dma((pieces, chips - 1)), dma((pieces, chips - 1)),
                dma((pieces,)), dma((pieces,)),
                dma((pieces, chips - 1)), dma((pieces, chips - 1)),
                dma((pieces,)),
                dma((n_z - 1,)), dma((n_z - 1,)),
                dma((n_z,)), dma((n_z,)),
                dma((2, n_z)), dma((2, n_z)),
                dma, dma((groups,)),
            ],
            compiler_params=pltpu.CompilerParams(
                collective_id=0, has_side_effects=True, vmem_limit_bytes=67_043_328 - 4 * momentum.size
            ),
        )(grad_block, momentum, model_root.reshape(2, half, width), expert_root)

    placed = (P("exp", "blk", None), P("exp", "blk", None), P("blk", None), P())
    return jax.shard_map(
        per_device, mesh=mesh, in_specs=placed, out_specs=P("exp", "blk", None), check_vma=False
    )
```

```python
import functools

import jax
import jax.numpy as jnp
from jax import lax
from jax.experimental import pallas as pl
from jax.experimental.pallas import tpu as pltpu
from jax.sharding import PartitionSpec as P

MESH = pl.DeviceIdType.MESH
SUB = 16
TILE = 256


def kernel(
    n_blk, n_exp, n_chunks,
    grad, momentum, root_rows, expert_hbm, out,
    expert_root, gathered, root, mix, blended,
    x_send, x_recv, p_send, p_recv, f_send, f_recv, own_sem,
    z_send, z_recv, y_send, y_recv, c_send, c_recv, root_sem, mom_sem, mix_sem,
):
    local_experts, local_hidden, width = grad.shape
    groups = local_hidden // SUB
    chunk = width // n_chunks
    chips = n_exp // 2
    n_z = n_blk // 2
    rows = local_experts * SUB
    half = root.shape[2]
    batch = 4 if n_exp % 4 == 0 else 2
    depth = batch * rows
    slice_rows = 2 * half

    me = lax.axis_index("exp")
    chip, core = me // 2, me % 2
    blk = lax.axis_index("blk")
    zi, yi = blk // 2, blk % 2
    mate = {"exp": chip * 2 + 1 - core}
    y_peer = {"blk": zi * 2 + 1 - yi}

    def chip_at(offset):
        return lax.rem(chip + offset + chips, chips)

    def z_at(offset):
        return lax.rem(zi + offset + n_z, n_z)

    def remote(src, dst, send, recv, device):
        return pltpu.make_async_remote_copy(
            src_ref=src, dst_ref=dst, send_sem=send, recv_sem=recv, device_id=device, device_id_type=MESH
        )

    barrier = pltpu.get_barrier_semaphore()
    peers = [mate, y_peer]
    peers += [{"exp": chip_at(c) * 2 + core} for c in range(1, chips)]
    peers += [{"blk": z_at(d) * 2 + yi} for d in range(1, n_z)]
    for peer in peers:
        pl.semaphore_signal(barrier, inc=1, device_id=peer, device_id_type=MESH)
    pl.semaphore_wait(barrier, len(peers))

    pieces = [(g, c) for g in range(groups) for c in range(n_chunks)]
    grad_at = [grad.at[:, pl.ds(g * SUB, SUB), pl.ds(c * chunk, chunk)] for g, c in pieces]

    def x_copy(p, off):
        slot = gathered.at[p, me]
        return remote(grad_at[p], slot, x_send.at[p, off - 1], x_recv.at[p, off - 1], {"exp": chip_at(off) * 2 + core})

    def p_copy(p):
        return remote(grad_at[p], gathered.at[p, me], p_send.at[p], p_recv.at[p], mate)

    def f_copy(p, off):
        slot = gathered.at[p, chip_at(-off) * 2 + core]
        return remote(slot, slot, f_send.at[p, off - 1], f_recv.at[p, off - 1], mate)

    def own_copy(p):
        return pltpu.make_async_copy(grad_at[p], gathered.at[p, me], own_sem.at[p])

    own_half = root_rows.at[core]

    def z_copy(d):
        return remote(own_half, root.at[blk, core], z_send.at[d - 1], z_recv.at[d - 1], {"blk": z_at(d) * 2 + yi})

    def y_copy(d):
        slot = root.at[z_at(-d) * 2 + yi, core]
        return remote(own_half if d == 0 else slot, slot, y_send.at[d], y_recv.at[d], y_peer)

    def c_copy(side, d):
        slot = root.at[z_at(-d) * 2 + (yi if side == 0 else 1 - yi), core]
        return remote(slot, slot, c_send.at[side, d], c_recv.at[side, d], mate)

    root_own = pltpu.make_async_copy(root_rows, root.at[blk], root_sem)

    def mom_copy(g):
        cols = pl.ds(g * SUB, SUB)
        return pltpu.make_async_copy(momentum.at[:, cols, :], out.at[:, cols, :], mom_sem.at[g])

    for off in range(1, chips):
        x_copy(0, off).start()
    y_copy(0).start()
    for d in range(1, n_z):
        z_copy(d).start()
    for p in range(1, len(pieces)):
        for off in range(1, chips):
            x_copy(p, off).start()
    take_mix = pltpu.make_async_copy(expert_hbm, expert_root, mix_sem)
    take_mix.start()
    for p in range(len(pieces)):
        own_copy(p).start()
        p_copy(p).start()
    root_own.start()
    for g in range(groups):
        mom_copy(g).start()

    take_mix.wait()
    experts = expert_root.shape[1]
    spread = lax.broadcasted_iota(jnp.int32, (rows, local_experts), 0) // SUB
    spread = spread == lax.broadcasted_iota(jnp.int32, (rows, local_experts), 1)
    mine = expert_root[pl.ds(pl.multiple_of(me * local_experts, local_experts), local_experts), :]
    tall = jnp.dot(jnp.where(spread, 1.0, 0.0).astype(jnp.bfloat16), mine, preferred_element_type=jnp.float32)
    tall = tall.astype(jnp.bfloat16)

    @pl.loop(0, experts * SUB // TILE)
    def _(t):
        col = t * TILE + lax.broadcasted_iota(jnp.int32, (experts, TILE), 1)
        pick = col // SUB == lax.broadcasted_iota(jnp.int32, (experts, TILE), 0)
        wide = jnp.dot(tall, jnp.where(pick, 1.0, 0.0).astype(jnp.bfloat16), preferred_element_type=jnp.float32)
        same = lax.broadcasted_iota(jnp.int32, (rows, TILE), 0) % SUB == lax.broadcasted_iota(
            jnp.int32, (rows, TILE), 1) % SUB
        mix[:, pl.ds(pl.multiple_of(t * TILE, TILE), TILE)] = jnp.where(same, wide, 0.0).astype(jnp.bfloat16)

    for g in range(groups):
        mom_copy(g).wait()

        @pl.loop(0, local_experts)
        def _(e):
            out[e, pl.ds(g * SUB, SUB)] = 0.9 * out[e, pl.ds(g * SUB, SUB)]

    def blend(p):
        g, c = pieces[p]

        @pl.loop(0, chunk // TILE)
        def _(t):
            lanes = pl.ds(pl.multiple_of(t * TILE, TILE), TILE)
            cols = pl.ds(pl.multiple_of(c * chunk + t * TILE, TILE), TILE)

            def term(k):
                block = gathered[p, pl.ds(k * batch, batch), :, :, lanes].reshape(depth, TILE)
                taps = mix[:, pl.ds(pl.multiple_of(k * depth, depth), depth)]
                return jnp.dot(taps, block, preferred_element_type=jnp.float32)

            acc = term(0)
            if n_exp > batch:
                acc = lax.fori_loop(1, n_exp // batch, lambda k, a: a + term(k), acc)
            blended[g, :, cols] = acc.astype(jnp.bfloat16)

    def apply_root(g, first, last):
        cols = pl.ds(first * chunk, (last - first) * chunk)

        @pl.loop(0, n_blk)
        def _(b):
            taps = root[b, :, :, cols].reshape(slice_rows, (last - first) * chunk)
            part = lax.dot_general(
                blended[g, :, cols], taps, (((1,), (1,)), ((), ())), preferred_element_type=jnp.float32
            )
            dst = pl.ds(pl.multiple_of(b * slice_rows, slice_rows), slice_rows)
            out[:, pl.ds(g * SUB, SUB), dst] += part.reshape(local_experts, SUB, slice_rows)

    def take_z(d):
        z_copy(d).wait_recv()
        y_copy(d).start()
        c_copy(0, d).start()

    def take_y(d):
        y_copy(d).wait_recv()
        c_copy(1, d).start()

    events = [functools.partial(take_z, d) for d in range(1, n_z)]
    events += [functools.partial(take_y, d) for d in range(n_z)]
    ready = len(pieces) * 11 // 16
    done = 0
    pending = 0
    for p, (g, c) in enumerate(pieces):
        for off in range(1, chips):
            x_copy(p, off).wait_recv()
            f_copy(p, off).start()
        goal = len(events) if p >= ready else len(events) * (p + 1) // (ready + 1)
        for event in events[done:goal]:
            event()
        done = goal
        own_copy(p).wait()
        p_copy(p).wait_recv()
        for off in range(1, chips):
            f_copy(p, off).wait_recv()
        blend(p)
        if p == ready:
            root_own.wait()
            for d in range(n_z):
                if d:
                    c_copy(0, d).wait_recv()
                c_copy(1, d).wait_recv()
        if p >= ready and p != len(pieces) - 3:
            while pending <= p and (p > ready or pieces[pending][0] < g):
                gg, first = pieces[pending]
                last = c + 1 if gg == g else n_chunks
                apply_root(gg, first, last)
                pending += last - first

    for p in range(len(pieces)):
        p_copy(p).wait_send()
        for off in range(1, chips):
            x_copy(p, off).wait_send()
            f_copy(p, off).wait_send()
    for d in range(n_z):
        y_copy(d).wait_send()
        c_copy(1, d).wait_send()
        if d:
            z_copy(d).wait_send()
            c_copy(0, d).wait_send()


def solution(mesh):
    n_blk, n_exp = mesh.shape["blk"], mesh.shape["exp"]

    def per_device(grad_block, momentum, model_root, expert_root):
        local_experts, local_hidden, width = grad_block.shape
        experts = expert_root.shape[0]
        groups, n_chunks = local_hidden // SUB, 8
        pieces, rows = groups * n_chunks, local_experts * SUB
        half = model_root.shape[0] // 2
        chips, n_z = n_exp // 2, n_blk // 2
        dma = pltpu.SemaphoreType.DMA
        hbm = pl.BlockSpec(memory_space=pl.ANY)
        return pl.pallas_call(
            functools.partial(kernel, n_blk, n_exp, n_chunks),
            out_shape=pltpu.VMEM(momentum.shape, jnp.float32),
            in_specs=[hbm] * 4,
            out_specs=pl.BlockSpec(memory_space=pltpu.VMEM),
            scratch_shapes=[
                pltpu.VMEM(expert_root.shape, jnp.bfloat16),
                pltpu.VMEM((pieces, n_exp, local_experts, SUB, width // n_chunks), jnp.bfloat16),
                pltpu.VMEM((n_blk, 2, half, width), jnp.bfloat16),
                pltpu.VMEM((rows, experts * SUB), jnp.bfloat16),
                pltpu.VMEM((groups, rows, width), jnp.bfloat16),
                dma((pieces, chips - 1)), dma((pieces, chips - 1)),
                dma((pieces,)), dma((pieces,)),
                dma((pieces, chips - 1)), dma((pieces, chips - 1)),
                dma((pieces,)),
                dma((n_z - 1,)), dma((n_z - 1,)),
                dma((n_z,)), dma((n_z,)),
                dma((2, n_z)), dma((2, n_z)),
                dma, dma((groups,)), dma,
            ],
            compiler_params=pltpu.CompilerParams(
                collective_id=0, has_side_effects=True, vmem_limit_bytes=67_043_328 - 4 * momentum.size
            ),
        )(grad_block, momentum, model_root.reshape(2, half, width), expert_root)

    placed = (P("exp", "blk", None), P("exp", "blk", None), P("blk", None), P())
    return jax.shard_map(
        per_device, mesh=mesh, in_specs=placed, out_specs=P("exp", "blk", None), check_vma=False
    )
```
